32 devices in a mesh: section: 2 (over core), dp: 4 (over z), expert: 4 (over y, x).
Axes of the slice: x: 2, y: 2, z: 4, core: 2. Of those that a mesh axis runs over, the one named last changes fastest.
Arguments:
- boundary_in: float32 [2, 2, 16, 197, 768], P('section', None, ('dp', 'expert')), may hold values from -6 to 6
- routes: int32 [2, 2, 16, 197, 2], P('section', None, ('dp', 'expert')), may hold values from 0 to 7, as said below
- capacity_slots: int32 [2, 2, 16, 197, 2], P('section', None, ('dp', 'expert')), may hold values from 0 to 40, as said below
- ln_gain: bfloat16 [2, 2, 768], P('section', None, ('dp', 'expert')), may hold values from 0.5 to 1.5
- ln_bias: bfloat16 [2, 2, 768], P('section', None, ('dp', 'expert')), may hold values from -3 to 3
- w_qkv: bfloat16 [2, 768, 2304], P('section', ('dp', 'expert')), may hold values from -0.21875 to 0.21875
- w_out: bfloat16 [2, 768, 768], P('section', ('dp', 'expert')), may hold values from -1.25 to 1.25
- w_router: bfloat16 [2, 768, 8], P('section', ('dp', 'expert')), may hold values from -0.21875 to 0.21875
- w_up: bfloat16 [2, 8, 768, 3072], P('section', 'expert', None, 'dp'), may hold values from -0.21875 to 0.21875
- w_down: bfloat16 [2, 8, 3072, 768], P('section', 'expert', 'dp'), may hold values from -0.109375 to 0.109375
Outputs:
- boundary_out: float32 [2, 2, 16, 197, 768], P('section', None, ('dp', 'expert'))
- grad_ln_gain: float32 [2, 2, 768], P('section', None, ('dp', 'expert'))
- grad_ln_bias: float32 [2, 2, 768], P('section', None, ('dp', 'expert'))
- grad_qkv: float32 [2, 768, 2304], P('section', ('dp', 'expert'))
- grad_out: float32 [2, 768, 768], P('section', ('dp', 'expert'))
- grad_router: float32 [2, 768, 8], P('section', ('dp', 'expert'))
- grad_up: float32 [2, 8, 768, 3072], P('section', 'expert', None, 'dp')
- grad_down: float32 [2, 8, 3072, 768], P('section', 'expert', 'dp')
The draws below stay inside these ranges and needn't reach their ends.
Inputs may be any that keep to these rules, and one draw needn't show every extreme that they name: `routes`: each token names two different experts of the 8. In every block (the 1 images of one micro-batch on one device of dp+expert, each layer apart) some expert is named by 40 or more tokens. `capacity_slots`: within a block, the kept choices of one expert hold the slots 0, 1, 2, ... without gaps or repeats; the value 40 marks a dropped choice, and every block drops at least one choice.
All inputs are finite; a program needn't handle non-finite values.
Results may differ from the reference program's by a relative error of at most 0.02.
Values may be sent and summed in bfloat16 or wider, within the bound.
A program may use at most 256 MiB of HBM per device.

```python
import math
import jax
import jax.numpy as jnp
from jax import lax

D = 768
HEADS = 12
HEAD_DIM = 64
FF = 3072
SEQ = 197
MB = 2
IMG_DEV = 1
LAYERS = 2
EXPERTS = 8
IMAGES = 16
CAP = 40


def routing(key):
    key_list = jax.random.split(jax.random.fold_in(key, 11), 5)
    block_count = IMAGES // IMG_DEV
    block_rows = IMG_DEV * SEQ
    shape = (LAYERS, MB, block_count, block_rows)
    weights = jax.random.randint(key_list[0], (LAYERS, EXPERTS), 1, 9, dtype=jnp.int32)
    bounds = jnp.cumsum(weights, axis=1)
    totals = bounds[:, -1]
    draws = jax.random.randint(key_list[1], shape, 0, 1 << 20, dtype=jnp.int32)
    target = draws % totals[:, None, None, None]
    first_ids = jnp.sum((target[..., None] >= bounds[:, None, None, None, :]).astype(jnp.int32), axis=-1)
    heavy = jax.random.randint(key_list[2], (LAYERS,), 0, EXPERTS, dtype=jnp.int32)
    position = jnp.arange(block_rows, dtype=jnp.int32)
    first_ids = jnp.where(position < CAP, heavy[:, None, None, None], first_ids)
    offsets = jax.random.randint(key_list[3], shape, 1, EXPERTS, dtype=jnp.int32)
    second_ids = (first_ids + offsets) % EXPERTS
    chosen = jnp.stack([first_ids, second_ids], axis=-1)
    flat = chosen.reshape(LAYERS, MB, block_count, 2 * block_rows)
    ranking = jax.random.randint(key_list[4], flat.shape, 0, 1 << 16, dtype=jnp.int32) * (2 * block_rows)
    ranking = ranking + jnp.arange(2 * block_rows, dtype=jnp.int32)
    order = jnp.argsort(ranking, axis=-1, stable=True)
    ordered = jnp.take_along_axis(flat, order, axis=-1)
    hits = (ordered[..., None] == jnp.arange(EXPERTS, dtype=jnp.int32)).astype(jnp.int32)
    before = jnp.cumsum(hits, axis=-2) - hits
    rank_sorted = jnp.sum(before * hits, axis=-1)
    inverse = jnp.argsort(order, axis=-1, stable=True)
    ranks = jnp.take_along_axis(rank_sorted, inverse, axis=-1)
    slot_values = jnp.minimum(ranks, CAP)
    return (chosen.reshape(LAYERS, MB, IMAGES, SEQ, 2), slot_values.reshape(LAYERS, MB, IMAGES, SEQ, 2))


def draw_routes(key, part):
    return routing(key)[0]


def draw_capacity_slots(key, part):
    return routing(key)[1]


def block_scale(stream_key, extent, cuts, least, largest):
    loudness, own = 1.0, jax.random.fold_in(stream_key, 6)
    for dim, shards_of in cuts:
        steps = jnp.exp(jax.random.uniform(jax.random.fold_in(own, dim), (shards_of,), jnp.float32, least / len(cuts), largest / len(cuts)))
        loudness = loudness * jnp.repeat(steps, extent[dim] // shards_of).reshape([-1 if axis == dim else 1 for axis in range(len(extent))])
    return loudness


def scatter_about(own_key, extent, scale, reach, pieces=(), held_as=jnp.bfloat16):
    drawn = jax.random.normal(own_key, extent, jnp.float32) * scale
    if len(pieces) > 0:
        drawn = block_scale(own_key, extent, pieces, -0.22, 0.18) * drawn
    return jnp.clip(drawn, min=-reach, max=reach).astype(held_as)


def setup_inputs(seed: int = 0) -> dict:
    streams_of = jax.random.split(jax.random.key(seed), 11)
    return {
        "boundary_in": scatter_about(streams_of[0], (2, MB, IMAGES, SEQ, D), 1.0, 6.0, ((0, 2), (2, 16)), jnp.float32),
        "routes": draw_routes(jax.random.fold_in(streams_of[10], 71), 0),
        "capacity_slots": draw_capacity_slots(jax.random.fold_in(streams_of[10], 71), 0),
        "ln_gain": jnp.clip(1.0 + 0.1 * jax.random.normal(streams_of[3], (LAYERS, 2, D), jnp.float32), 0.5, 1.5).astype(jnp.bfloat16),
        "ln_bias": scatter_about(streams_of[4], (LAYERS, 2, D), 0.5, 3.0, ((0, 2), (2, 16))),
        "w_qkv": scatter_about(streams_of[5], (LAYERS, D, 3 * D), D ** -0.5, 0.21875, ((0, 2), (1, 16))),
        "w_out": scatter_about(streams_of[6], (LAYERS, D, D), (D // 32) ** -0.5, 1.25, ((0, 2), (1, 16))),
        "w_router": scatter_about(streams_of[7], (LAYERS, D, EXPERTS), D ** -0.5, 0.21875, ((0, 2), (1, 16))),
        "w_up": scatter_about(streams_of[8], (LAYERS, EXPERTS, D, FF), D ** -0.5, 0.21875, ((0, 2), (1, 4), (3, 4))),
        "w_down": scatter_about(streams_of[9], (LAYERS, EXPERTS, FF, D), FF ** -0.5, 0.109375, ((0, 2), (1, 4), (2, 4))),
    }


EPS = 1e-06
SQRT_HALF = 0.7071067811865476
INV_ROOT_TAU = 0.3989422804014327

def norm_forward(values, gain_row, shift_row):
    centred = values - lax.optimization_barrier(jnp.mean(values, axis=-1, keepdims=True))
    variance = lax.optimization_barrier(jnp.mean(centred * centred, axis=-1, keepdims=True))
    inverse = lax.rsqrt(variance + EPS)
    unit_rows = centred * inverse
    return (unit_rows * gain_row + shift_row, unit_rows, inverse)

def norm_backward(d_normed, unit_rows, inverse, gain_row):
    d_gain = lax.optimization_barrier(jnp.sum(d_normed * unit_rows, axis=0))
    d_shift = lax.optimization_barrier(jnp.sum(d_normed, axis=0))
    scaled = d_normed * gain_row
    d_values = inverse * (scaled - lax.optimization_barrier(jnp.mean(scaled, axis=-1, keepdims=True)) - unit_rows * lax.optimization_barrier(jnp.mean(scaled * unit_rows, axis=-1, keepdims=True)))
    return (d_values, d_gain, d_shift)

def gelu_slope(pre_act):
    return 0.5 * (1.0 + lax.erf(pre_act * SQRT_HALF)) + pre_act * jnp.exp(-0.5 * pre_act * pre_act) * INV_ROOT_TAU

def split_heads(qkv_rows, image_count):
    feature_count = qkv_rows.shape[1] // 3
    return [qkv_rows[:, part_index * feature_count:(part_index + 1) * feature_count].astype(jnp.float32).reshape(image_count, SEQ, HEADS, HEAD_DIM) for part_index in range(3)]

def attend_forward(qkv_rows, image_count):
    queries, key_rows, value_rows = split_heads(qkv_rows, image_count)
    scale_factor = 1.0 / math.sqrt(HEAD_DIM)
    scores = jnp.einsum('bqhd,bkhd->bhqk', queries, key_rows) * scale_factor
    log_totals = jnp.log(lax.optimization_barrier(jnp.sum(jnp.exp(scores), axis=-1)))
    probs_half = jnp.exp(scores - log_totals[..., None]).astype(jnp.bfloat16)
    attended = jnp.einsum('bhqk,bkhd->bqhd', probs_half.astype(jnp.float32), value_rows)
    return (attended.astype(jnp.bfloat16).reshape(-1, HEADS * HEAD_DIM), log_totals)

def attend_backward(qkv_rows, log_totals, d_attended, image_count):
    queries, key_rows, value_rows = split_heads(qkv_rows, image_count)
    scale_factor = 1.0 / math.sqrt(HEAD_DIM)
    scores = jnp.einsum('bqhd,bkhd->bhqk', queries, key_rows) * scale_factor
    probs = jnp.exp(scores - log_totals[..., None])
    probs_half = probs.astype(jnp.bfloat16).astype(jnp.float32)
    d_heads = d_attended.astype(jnp.float32).reshape(image_count, SEQ, HEADS, HEAD_DIM)
    d_values = jnp.einsum('bhqk,bqhd->bkhd', probs_half, d_heads)
    d_probs = jnp.einsum('bqhd,bkhd->bhqk', d_heads, value_rows)
    row_dot = lax.optimization_barrier(jnp.sum(probs * d_probs, axis=-1, keepdims=True))
    d_scores = (probs * (d_probs - row_dot) * scale_factor).astype(jnp.bfloat16).astype(jnp.float32)
    d_queries = jnp.einsum('bhqk,bkhd->bqhd', d_scores, key_rows)
    d_keys = jnp.einsum('bhqk,bqhd->bkhd', d_scores, queries)
    feature_count = HEADS * HEAD_DIM
    joined = jnp.concatenate([d_queries.reshape(-1, feature_count), d_keys.reshape(-1, feature_count), d_values.reshape(-1, feature_count)], axis=1)
    return joined.astype(jnp.bfloat16)

def to_experts(blocked):
    block_count = blocked.shape[0]
    grouped = blocked.reshape(block_count, EXPERTS, CAP, blocked.shape[-1])
    return jnp.transpose(grouped, (1, 0, 2, 3)).reshape(EXPERTS, block_count * CAP, blocked.shape[-1])

def from_experts(rows_by_expert, block_count):
    grouped = rows_by_expert.reshape(EXPERTS, block_count, CAP, rows_by_expert.shape[-1])
    return jnp.transpose(grouped, (1, 0, 2, 3)).reshape(block_count, EXPERTS * CAP, rows_by_expert.shape[-1])

def tables(expert_ids, slot_ids):
    slot_index = jnp.where(slot_ids < CAP, expert_ids * CAP + slot_ids, -1)
    onehot = (slot_index[..., None] == jnp.arange(EXPERTS * CAP, dtype=jnp.int32)).astype(jnp.float32)
    chosen = (expert_ids[..., None] == jnp.arange(EXPERTS, dtype=jnp.int32)).astype(jnp.float32)
    return (onehot, chosen)

def layer_forward(inputs, params, expert_ids, slot_ids):
    gain_rows, shift_rows, weight_qkv, weight_out, weight_router, weight_up, weight_down = params
    block_count, block_rows = (expert_ids.shape[0], expert_ids.shape[1])
    normed_one, unit_one, inverse_one = norm_forward(inputs, gain_rows[0], shift_rows[0])
    norm_one = normed_one.astype(jnp.bfloat16)
    qkv_rows = jnp.dot(norm_one, weight_qkv, preferred_element_type=jnp.float32).astype(jnp.bfloat16)
    attended, log_totals = attend_forward(qkv_rows, IMAGES)
    middle = inputs + jnp.dot(attended, weight_out, preferred_element_type=jnp.float32)
    normed_two, unit_two, inverse_two = norm_forward(middle, gain_rows[1], shift_rows[1])
    norm_two = normed_two.astype(jnp.bfloat16)
    logits = jnp.dot(norm_two, weight_router, preferred_element_type=jnp.float32).reshape(block_count, block_rows, EXPERTS)
    onehot, chosen = tables(expert_ids, slot_ids)
    picked = lax.optimization_barrier(jnp.sum(logits[:, :, None, :] * chosen, axis=-1))
    leading = jax.nn.sigmoid(picked[..., 0] - picked[..., 1])
    gate_pair = jnp.stack([leading, 1.0 - leading], axis=-1)
    norm_blocks = norm_two.reshape(block_count, block_rows, -1).astype(jnp.float32)
    buffer = jnp.einsum('btjs,btd->bsd', onehot, norm_blocks).astype(jnp.bfloat16)
    inbound = to_experts(buffer)
    pre_act = jnp.einsum('erd,edf->erf', inbound.astype(jnp.float32), weight_up.astype(jnp.float32))
    hidden = jax.nn.gelu(pre_act, approximate=False).astype(jnp.bfloat16)
    results = jnp.einsum('erf,efd->erd', hidden.astype(jnp.float32), weight_down.astype(jnp.float32)).astype(jnp.bfloat16)
    back_rows = from_experts(results, block_count)
    selected = jnp.einsum('btjs,bsd->btjd', onehot, back_rows.astype(jnp.float32))
    out_rows = middle + lax.optimization_barrier(jnp.sum(gate_pair[..., None] * selected, axis=2)).reshape(middle.shape)
    saved = (unit_one, inverse_one, norm_one, qkv_rows, log_totals, attended, unit_two, inverse_two, norm_two, gate_pair, selected, inbound, pre_act, hidden)
    return (out_rows, saved)

def layer_backward(d_out, saved, params, expert_ids, slot_ids):
    gain_rows, shift_rows, weight_qkv, weight_out, weight_router, weight_up, weight_down = params
    unit_one, inverse_one, norm_one, qkv_rows, log_totals, attended, unit_two, inverse_two, norm_two, gate_pair, selected, inbound, pre_act, hidden = saved
    block_count, block_rows = (expert_ids.shape[0], expert_ids.shape[1])
    onehot, chosen = tables(expert_ids, slot_ids)
    d_blocks = d_out.reshape(block_count, block_rows, -1)
    d_gate = lax.optimization_barrier(jnp.sum(d_blocks[:, :, None, :] * selected, axis=-1))
    d_lead = (d_gate[..., 0] - d_gate[..., 1]) * gate_pair[..., 0] * gate_pair[..., 1]
    d_logits = (d_lead[..., None] * (chosen[:, :, 0, :] - chosen[:, :, 1, :])).astype(jnp.bfloat16).reshape(-1, EXPERTS)
    router_grad = jnp.einsum('td,te->de', norm_two.astype(jnp.float32), d_logits.astype(jnp.float32))
    weighted = gate_pair[..., None] * d_blocks[:, :, None, :]
    d_buffer = jnp.einsum('btjs,btjd->bsd', onehot, weighted, precision=lax.Precision.HIGHEST).astype(jnp.bfloat16)
    d_results = to_experts(d_buffer).astype(jnp.float32)
    down_grad = jnp.einsum('erf,erd->efd', hidden.astype(jnp.float32), d_results)
    d_hidden = jnp.einsum('erd,efd->erf', d_results, weight_down.astype(jnp.float32))
    d_pre = (d_hidden * gelu_slope(pre_act)).astype(jnp.bfloat16).astype(jnp.float32)
    up_grad = jnp.einsum('erd,erf->edf', inbound.astype(jnp.float32), d_pre)
    d_inbound = jnp.einsum('erf,edf->erd', d_pre, weight_up.astype(jnp.float32)).astype(jnp.bfloat16)
    d_back = from_experts(d_inbound, block_count).astype(jnp.float32)
    d_norm_two = jnp.einsum('btjs,bsd->btd', onehot, d_back).reshape(d_out.shape)
    d_norm_two = d_norm_two + jnp.dot(d_logits, weight_router.T, preferred_element_type=jnp.float32)
    d_middle_norm, gain_two, shift_two = norm_backward(d_norm_two, unit_two, inverse_two, gain_rows[1])
    d_middle = d_out + d_middle_norm
    d_middle_half = d_middle.astype(jnp.bfloat16)
    out_grad = jnp.einsum('td,te->de', attended.astype(jnp.float32), d_middle_half.astype(jnp.float32))
    d_attended = jnp.dot(d_middle_half, weight_out.T, preferred_element_type=jnp.float32).astype(jnp.bfloat16)
    d_qkv = attend_backward(qkv_rows, log_totals, d_attended, IMAGES)
    qkv_grad = jnp.einsum('td,te->de', norm_one.astype(jnp.float32), d_qkv.astype(jnp.float32))
    d_norm_one = jnp.dot(d_qkv, weight_qkv.T, preferred_element_type=jnp.float32)
    d_input_norm, gain_one, shift_one = norm_backward(d_norm_one, unit_one, inverse_one, gain_rows[0])
    d_input = d_middle + d_input_norm
    grads = (jnp.stack([gain_one, gain_two]), jnp.stack([shift_one, shift_two]), qkv_grad, out_grad, router_grad, up_grad, down_grad)
    return (d_input, grads)

def round_trip(values):
    return lax.optimization_barrier(values.astype(jnp.bfloat16)).astype(jnp.float32)

def reference(boundary_in, routes, capacity_slots, ln_gain, ln_bias, w_qkv, w_out, w_router, w_up, w_down):
    block_count = IMAGES // IMG_DEV
    block_rows = IMG_DEV * SEQ
    layer_params = [(ln_gain[layer_index].astype(jnp.float32), ln_bias[layer_index].astype(jnp.float32), w_qkv[layer_index], w_out[layer_index], w_router[layer_index], w_up[layer_index], w_down[layer_index]) for layer_index in range(LAYERS)]
    grad_totals = [None for layer_index in range(LAYERS)]
    input_grads = []
    layer_outputs = []
    for micro_index in range(MB):
        route_now = [routes[layer_index, micro_index].reshape(block_count, block_rows, 2) for layer_index in range(LAYERS)]
        slot_now = [capacity_slots[layer_index, micro_index].reshape(block_count, block_rows, 2) for layer_index in range(LAYERS)]
        stream = boundary_in[0, micro_index].reshape(-1, D)
        saved_list = []
        for layer_index in range(LAYERS):
            if layer_index > 0:
                stream = round_trip(stream)
            stream, saved = layer_forward(stream, layer_params[layer_index], route_now[layer_index], slot_now[layer_index])
            saved_list.append(saved)
        layer_outputs.append(stream)
        cotangent = boundary_in[1, micro_index].reshape(-1, D)
        for layer_index in reversed(range(LAYERS)):
            if layer_index < LAYERS - 1:
                cotangent = round_trip(cotangent)
            cotangent, grads = layer_backward(cotangent, saved_list[layer_index], layer_params[layer_index], route_now[layer_index], slot_now[layer_index])
            if grad_totals[layer_index] is None:
                grad_totals[layer_index] = grads
            else:
                grad_totals[layer_index] = jax.tree.map(jnp.add, grad_totals[layer_index], grads)
        input_grads.append(cotangent)
    boundary_out = jnp.stack([jnp.stack(input_grads), jnp.stack(layer_outputs)]).reshape(2, MB, IMAGES, SEQ, D)
    stacked = [jnp.stack([grad_totals[layer_index][part_index] for layer_index in range(LAYERS)]) for part_index in range(7)]
    return (boundary_out, stacked[0], stacked[1], stacked[2], stacked[3], stacked[4], stacked[5], stacked[6])
```

```python
import math

import jax
import jax.numpy as jnp
from jax import lax
from jax.sharding import PartitionSpec as P

HEADS = 12
HEAD_DIM = 64
EXP_DEV = 2
MB = 2


EPS = 1e-06
SQRT_HALF = 0.7071067811865476
INV_ROOT_TAU = 0.3989422804014327


def norm_forward(values, gain_row, shift_row):
    centred = values - jnp.mean(values, axis=-1, keepdims=True)
    variance = jnp.mean(centred * centred, axis=-1, keepdims=True)
    inverse = lax.rsqrt(variance + EPS)
    unit_rows = centred * inverse
    return (unit_rows * gain_row + shift_row, unit_rows, inverse)


def norm_backward(d_normed, unit_rows, inverse, gain_row):
    d_gain = jnp.sum(d_normed * unit_rows, axis=0)
    d_shift = jnp.sum(d_normed, axis=0)
    scaled = d_normed * gain_row
    d_values = inverse * (
        scaled
        - jnp.mean(scaled, axis=-1, keepdims=True)
        - unit_rows * jnp.mean(scaled * unit_rows, axis=-1, keepdims=True)
    )
    return (d_values, d_gain, d_shift)


def gelu_slope(pre_act):
    return (
        0.5 * (1.0 + lax.erf(pre_act * SQRT_HALF))
        + pre_act * jnp.exp(-0.5 * pre_act * pre_act) * INV_ROOT_TAU
    )


def split_heads(qkv_rows, image_count):
    feature_count = qkv_rows.shape[1] // 3
    return [
        qkv_rows[:, part_index * feature_count : (part_index + 1) * feature_count].reshape(
            image_count, -1, HEADS, HEAD_DIM
        )
        for part_index in range(3)
    ]


def attend_forward(qkv_rows, image_count):
    queries, key_rows, value_rows = split_heads(qkv_rows, image_count)
    scale_factor = 1.0 / math.sqrt(HEAD_DIM)
    scores = (
        jnp.einsum("bqhd,bkhd->bhqk", queries, key_rows, preferred_element_type=jnp.float32)
        * scale_factor
    )
    log_totals = jnp.log(jnp.sum(jnp.exp(scores), axis=-1))
    probs_half = jnp.exp(scores - log_totals[..., None]).astype(jnp.bfloat16)
    attended = jnp.einsum(
        "bhqk,bkhd->bqhd", probs_half, value_rows, preferred_element_type=jnp.float32
    )
    return (attended.astype(jnp.bfloat16).reshape(-1, HEADS * HEAD_DIM), log_totals)


def attend_backward(qkv_rows, log_totals, d_attended, image_count):
    queries, key_rows, value_rows = split_heads(qkv_rows, image_count)
    scale_factor = 1.0 / math.sqrt(HEAD_DIM)
    scores = (
        jnp.einsum("bqhd,bkhd->bhqk", queries, key_rows, preferred_element_type=jnp.float32)
        * scale_factor
    )
    probs = jnp.exp(scores - log_totals[..., None])
    probs_half = probs.astype(jnp.bfloat16)
    d_heads = d_attended.reshape(image_count, -1, HEADS, HEAD_DIM)
    d_values = jnp.einsum(
        "bhqk,bqhd->bkhd", probs_half, d_heads, preferred_element_type=jnp.float32
    )
    d_probs = jnp.einsum("bqhd,bkhd->bhqk", d_heads, value_rows, preferred_element_type=jnp.float32)
    row_dot = jnp.sum(probs * d_probs, axis=-1, keepdims=True)
    d_scores = (probs * (d_probs - row_dot) * scale_factor).astype(jnp.bfloat16)
    d_queries = jnp.einsum(
        "bhqk,bkhd->bqhd", d_scores, key_rows, preferred_element_type=jnp.float32
    )
    d_keys = jnp.einsum("bhqk,bqhd->bkhd", d_scores, queries, preferred_element_type=jnp.float32)
    feature_count = HEADS * HEAD_DIM
    joined = jnp.concatenate(
        [
            d_queries.reshape(-1, feature_count),
            d_keys.reshape(-1, feature_count),
            d_values.reshape(-1, feature_count),
        ],
        axis=1,
    )
    return joined.astype(jnp.bfloat16)


def on_device(
    boundary_in, routes, capacity_slots, ln_gain, ln_bias, w_qkv, w_out, w_router, w_up, w_down
):
    section_index = lax.axis_index("section")
    is_first = section_index == 0
    expert_count = EXP_DEV * lax.axis_size("expert")
    local_images = boundary_in.shape[2]
    token_rows = local_images * boundary_in.shape[3]
    model_width = boundary_in.shape[4]
    capacity = 26 * token_rows // (16 * expert_count)
    chips = ("dp", "expert")
    half = jnp.bfloat16

    def by_micro(values):
        return lax.all_to_all(values, "section", split_axis=0, concat_axis=0, tiled=True)

    edge_rows = by_micro(boundary_in[0].reshape(MB, token_rows, model_width))
    route_rows = by_micro(routes[0].reshape(MB, token_rows, 2))
    slot_rows = by_micro(capacity_slots[0].reshape(MB, token_rows, 2))

    def both_layers(shard, axis):
        whole = lax.all_gather(shard, chips, axis=axis, tiled=True)
        return lax.all_gather(whole, "section", axis=0, tiled=True)

    gain_all = both_layers(ln_gain, 2).astype(jnp.float32)
    shift_all = both_layers(ln_bias, 2).astype(jnp.float32)
    qkv_all = both_layers(w_qkv, 1)
    out_all = both_layers(w_out, 1)
    router_all = both_layers(w_router, 1)
    up_all = lax.all_gather(w_up, "section", axis=0, tiled=True)
    down_all = lax.all_gather(w_down, "section", axis=0, tiled=True)

    def tables(expert_ids, slot_ids):
        slot_index = jnp.where(slot_ids < capacity, expert_ids * capacity + slot_ids, -1)
        columns = jnp.arange(expert_count * capacity, dtype=jnp.int32)
        onehot = (slot_index[:, :, None] == columns).astype(half)
        chosen = (expert_ids[:, :, None] == jnp.arange(expert_count, dtype=jnp.int32)).astype(
            jnp.float32
        )
        return (onehot, chosen)

    def to_experts(rows):
        blocks = rows.reshape(expert_count, capacity, model_width)
        arrived = lax.all_to_all(blocks, "expert", split_axis=0, concat_axis=1, tiled=True)
        return lax.all_gather(arrived, "dp", axis=1, tiled=True)

    def from_experts(partial):
        pieces = lax.all_to_all(
            partial.astype(half)[None], "dp", split_axis=2, concat_axis=0, tiled=True
        )
        total = jnp.sum(pieces.astype(jnp.float32), axis=0).astype(half)
        return lax.all_to_all(
            total, "expert", split_axis=1, concat_axis=0, tiled=True
        ).reshape(expert_count * capacity, model_width)

    def layer_forward(layer, inputs):
        onehot, chosen = tables(route_rows[layer], slot_rows[layer])
        normed_one, unit_one, inverse_one = norm_forward(
            inputs, gain_all[layer, 0], shift_all[layer, 0]
        )
        norm_one = normed_one.astype(half)
        qkv_rows = jnp.dot(norm_one, qkv_all[layer], preferred_element_type=jnp.float32).astype(half)
        attended, log_totals = attend_forward(qkv_rows, local_images)
        middle = inputs + jnp.dot(attended, out_all[layer], preferred_element_type=jnp.float32)
        normed_two, unit_two, inverse_two = norm_forward(
            middle, gain_all[layer, 1], shift_all[layer, 1]
        )
        norm_two = normed_two.astype(half)
        logits = jnp.dot(norm_two, router_all[layer], preferred_element_type=jnp.float32)
        picked = jnp.sum(logits[:, None, :] * chosen, axis=-1)
        leading = jax.nn.sigmoid(picked[:, 0] - picked[:, 1])
        gate_pair = jnp.stack([leading, 1.0 - leading], axis=-1)
        buffer = jnp.einsum(
            "tjs,td->sd", onehot, norm_two, preferred_element_type=jnp.float32
        ).astype(half)
        all_rows = to_experts(buffer)
        pre_act = jnp.einsum(
            "erd,edf->erf", all_rows, up_all[layer], preferred_element_type=jnp.float32
        )
        hidden = jax.nn.gelu(pre_act, approximate=False).astype(half)
        partial_out = jnp.einsum(
            "erf,efd->erd", hidden, down_all[layer], preferred_element_type=jnp.float32
        )
        back_rows = from_experts(partial_out)
        selected = jnp.einsum(
            "tjs,sd->tjd", onehot, back_rows, preferred_element_type=jnp.float32
        )
        out_rows = middle + jnp.sum(gate_pair[:, :, None] * selected, axis=1)
        saved = (
            inputs, norm_one, qkv_rows, log_totals, attended, middle, norm_two, gate_pair,
            back_rows, all_rows, pre_act, hidden,
        )
        return (out_rows, saved)

    def layer_backward(layer, d_out, saved):
        (
            inputs, norm_one, qkv_rows, log_totals, attended, middle, norm_two, gate_pair,
            back_rows, all_rows, pre_act, hidden,
        ) = saved
        onehot, chosen = tables(route_rows[layer], slot_rows[layer])
        weighted = (gate_pair[:, :, None] * d_out[:, None, :]).astype(half)
        d_buffer = jnp.einsum(
            "tjs,tjd->sd", onehot, weighted, preferred_element_type=jnp.float32
        ).astype(half)
        grads_in = to_experts(d_buffer)
        selected = jnp.einsum("tjs,sd->tjd", onehot, back_rows, preferred_element_type=jnp.float32)
        d_gate = jnp.sum(d_out[:, None, :] * selected, axis=-1)
        d_lead = (d_gate[:, 0] - d_gate[:, 1]) * gate_pair[:, 0] * gate_pair[:, 1]
        d_logits = (d_lead[:, None] * (chosen[:, 0] - chosen[:, 1])).astype(half)
        d_hidden = jnp.einsum(
            "erd,efd->erf", grads_in, down_all[layer], preferred_element_type=jnp.float32
        )
        d_pre = (d_hidden * gelu_slope(pre_act)).astype(half)
        partial_in = jnp.einsum(
            "erf,edf->erd", d_pre, up_all[layer], preferred_element_type=jnp.float32
        )
        d_back = from_experts(partial_in)
        up_grad = jnp.einsum("erd,erf->edf", all_rows, d_pre, preferred_element_type=jnp.float32)
        down_grad = jnp.einsum(
            "erf,erd->efd", hidden, grads_in, preferred_element_type=jnp.float32
        )
        owner_pairs = [(1 - layer, layer)]
        up_sent = lax.ppermute(up_grad.astype(half), "section", owner_pairs)
        down_sent = lax.ppermute(down_grad.astype(half), "section", owner_pairs)
        d_norm_two = jnp.einsum("tjs,sd->td", onehot, d_back, preferred_element_type=jnp.float32)
        d_norm_two = d_norm_two + jnp.einsum(
            "te,de->td", d_logits, router_all[layer], preferred_element_type=jnp.float32
        )
        normed_two, unit_two, inverse_two = norm_forward(
            middle, gain_all[layer, 1], shift_all[layer, 1]
        )
        d_middle_norm, gain_two, shift_two = norm_backward(
            d_norm_two, unit_two, inverse_two, gain_all[layer, 1]
        )
        d_middle = d_out + d_middle_norm
        d_middle_half = d_middle.astype(half)
        d_attended = jnp.einsum(
            "te,de->td", d_middle_half, out_all[layer], preferred_element_type=jnp.float32
        ).astype(half)
        d_qkv = attend_backward(qkv_rows, log_totals, d_attended, local_images)
        d_norm_one = jnp.einsum(
            "te,de->td", d_qkv, qkv_all[layer], preferred_element_type=jnp.float32
        )
        normed_one, unit_one, inverse_one = norm_forward(
            inputs, gain_all[layer, 0], shift_all[layer, 0]
        )
        d_input_norm, gain_one, shift_one = norm_backward(
            d_norm_one, unit_one, inverse_one, gain_all[layer, 0]
        )
        d_input = d_middle + d_input_norm
        operands = [
            lax.ppermute(item, "section", owner_pairs)
            for item in (norm_one, d_qkv, attended, d_middle_half)
        ]
        own = (norm_one, d_qkv, attended, d_middle_half)
        small = jnp.concatenate(
            [
                jnp.stack([gain_one, gain_two, shift_one, shift_two]),
                jnp.einsum("td,te->ed", norm_two, d_logits, preferred_element_type=jnp.float32),
            ]
        )
        return (d_input, own, operands, small, (up_grad, up_sent), (down_grad, down_sent))

    stream = edge_rows[0]
    saved_list = []
    for layer in range(2):
        if layer > 0:
            stream = stream.astype(half).astype(jnp.float32)
        stream, saved = layer_forward(layer, stream)
        saved_list.append(saved)
    cotangent = edge_rows[1]
    parts = [None, None]
    for layer in (1, 0):
        if layer < 1:
            cotangent = cotangent.astype(half).astype(jnp.float32)
        cotangent, *parts[layer] = layer_backward(layer, cotangent, saved_list[layer])

    def mine(first, second):
        return jnp.where(is_first, first, second)

    own = [mine(a, b) for a, b in zip(parts[0][0], parts[1][0])]
    other = [mine(a, b) for a, b in zip(parts[0][1], parts[1][1])]
    pairs = [jnp.stack([a, b]) for a, b in zip(own, other)]
    qkv_grad = jnp.einsum("ktd,kte->de", pairs[0], pairs[1], preferred_element_type=jnp.float32)
    out_grad = jnp.einsum("ktd,kte->de", pairs[2], pairs[3], preferred_element_type=jnp.float32)
    small_both = lax.psum(jnp.stack([parts[0][2], parts[1][2]]), "section")
    small_mine = mine(small_both[0], small_both[1])
    small_shard = lax.psum_scatter(small_mine, chips, scatter_dimension=1, tiled=True)
    qkv_shard = lax.psum_scatter(qkv_grad, chips, scatter_dimension=0, tiled=True)
    out_shard = lax.psum_scatter(out_grad, chips, scatter_dimension=0, tiled=True)

    def expert_grad(index):
        first = parts[0][index][0] + parts[0][index][1].astype(jnp.float32)
        second = parts[1][index][0] + parts[1][index][1].astype(jnp.float32)
        return mine(first, second)[None]

    up_shard = expert_grad(3)
    down_shard = expert_grad(4)
    boundary_rows = by_micro(jnp.stack([cotangent, stream]))
    boundary_out = boundary_rows.reshape(1, MB, local_images, boundary_in.shape[3], model_width)
    return (
        boundary_out,
        small_shard[None, 0:2],
        small_shard[None, 2:4],
        qkv_shard[None],
        out_shard[None],
        small_shard[4:].T[None],
        up_shard,
        down_shard,
    )


def solution(mesh):
    in_specs = (
        P("section", None, ("dp", "expert"), None, None),
        P("section", None, ("dp", "expert"), None, None),
        P("section", None, ("dp", "expert"), None, None),
        P("section", None, ("dp", "expert")),
        P("section", None, ("dp", "expert")),
        P("section", ("dp", "expert"), None),
        P("section", ("dp", "expert"), None),
        P("section", ("dp", "expert"), None),
        P("section", "expert", None, "dp"),
        P("section", "expert", "dp", None),
    )
    out_specs = (
        P("section", None, ("dp", "expert"), None, None),
        P("section", None, ("dp", "expert")),
        P("section", None, ("dp", "expert")),
        P("section", ("dp", "expert"), None),
        P("section", ("dp", "expert"), None),
        P("section", ("dp", "expert"), None),
        P("section", "expert", None, "dp"),
        P("section", "expert", "dp", None),
    )
    return jax.shard_map(
        on_device, mesh=mesh, in_specs=in_specs, out_specs=out_specs, check_vma=False
    )
```

```python
import math

import jax
import jax.numpy as jnp
from jax import lax
from jax.sharding import PartitionSpec as P

HEADS = 12
HEAD_DIM = 64
EXP_DEV = 2
MB = 2


EPS = 1e-06
SQRT_HALF = 0.7071067811865476
INV_ROOT_TAU = 0.3989422804014327


def norm_forward(values, gain_row, shift_row):
    centred = values - jnp.mean(values, axis=-1, keepdims=True)
    variance = jnp.mean(centred * centred, axis=-1, keepdims=True)
    inverse = lax.rsqrt(variance + EPS)
    unit_rows = centred * inverse
    return (unit_rows * gain_row + shift_row, unit_rows, inverse)


def norm_backward(d_normed, unit_rows, inverse, gain_row):
    d_gain = jnp.sum(d_normed * unit_rows, axis=0)
    d_shift = jnp.sum(d_normed, axis=0)
    scaled = d_normed * gain_row
    d_values = inverse * (
        scaled
        - jnp.mean(scaled, axis=-1, keepdims=True)
        - unit_rows * jnp.mean(scaled * unit_rows, axis=-1, keepdims=True)
    )
    return (d_values, d_gain, d_shift)


def gelu_slope(pre_act):
    return (
        0.5 * (1.0 + lax.erf(pre_act * SQRT_HALF))
        + pre_act * jnp.exp(-0.5 * pre_act * pre_act) * INV_ROOT_TAU
    )


def split_heads(qkv_rows, image_count):
    feature_count = qkv_rows.shape[1] // 3
    return [
        qkv_rows[:, part_index * feature_count : (part_index + 1) * feature_count].reshape(
            image_count, -1, HEADS, HEAD_DIM
        )
        for part_index in range(3)
    ]


def attend_forward(qkv_rows, image_count):
    queries, key_rows, value_rows = split_heads(qkv_rows, image_count)
    scale_factor = 1.0 / math.sqrt(HEAD_DIM)
    scores = (
        jnp.einsum("bqhd,bkhd->bhqk", queries, key_rows, preferred_element_type=jnp.float32)
        * scale_factor
    )
    log_totals = jnp.log(jnp.sum(jnp.exp(scores), axis=-1))
    probs_half = jnp.exp(scores - log_totals[..., None]).astype(jnp.bfloat16)
    attended = jnp.einsum(
        "bhqk,bkhd->bqhd", probs_half, value_rows, preferred_element_type=jnp.float32
    )
    return (attended.astype(jnp.bfloat16).reshape(-1, HEADS * HEAD_DIM), log_totals)


def attend_backward(qkv_rows, log_totals, d_attended, image_count):
    queries, key_rows, value_rows = split_heads(qkv_rows, image_count)
    scale_factor = 1.0 / math.sqrt(HEAD_DIM)
    scores = (
        jnp.einsum("bqhd,bkhd->bhqk", queries, key_rows, preferred_element_type=jnp.float32)
        * scale_factor
    )
    probs = jnp.exp(scores - log_totals[..., None])
    probs_half = probs.astype(jnp.bfloat16)
    d_heads = d_attended.reshape(image_count, -1, HEADS, HEAD_DIM)
    d_values = jnp.einsum(
        "bhqk,bqhd->bkhd", probs_half, d_heads, preferred_element_type=jnp.float32
    )
    d_probs = jnp.einsum("bqhd,bkhd->bhqk", d_heads, value_rows, preferred_element_type=jnp.float32)
    row_dot = jnp.sum(probs * d_probs, axis=-1, keepdims=True)
    d_scores = (probs * (d_probs - row_dot) * scale_factor).astype(jnp.bfloat16)
    d_queries = jnp.einsum(
        "bhqk,bkhd->bqhd", d_scores, key_rows, preferred_element_type=jnp.float32
    )
    d_keys = jnp.einsum("bhqk,bqhd->bkhd", d_scores, queries, preferred_element_type=jnp.float32)
    feature_count = HEADS * HEAD_DIM
    joined = jnp.concatenate(
        [
            d_queries.reshape(-1, feature_count),
            d_keys.reshape(-1, feature_count),
            d_values.reshape(-1, feature_count),
        ],
        axis=1,
    )
    return joined.astype(jnp.bfloat16)


def on_device(
    boundary_in, routes, capacity_slots, ln_gain, ln_bias, w_qkv, w_out, w_router, w_up, w_down
):
    section_index = lax.axis_index("section")
    is_first = section_index == 0
    depth = lax.axis_size("dp")
    groups = lax.axis_size("expert")
    expert_count = EXP_DEV * groups
    local_images = boundary_in.shape[2]
    token_rows = local_images * boundary_in.shape[3]
    model_width = boundary_in.shape[4]
    capacity = 26 * token_rows // (16 * expert_count)
    chips = ("dp", "expert")
    half = jnp.bfloat16

    def by_micro(values):
        return lax.all_to_all(values, "section", split_axis=0, concat_axis=0, tiled=True)

    edge_rows = by_micro(boundary_in[0].reshape(MB, token_rows, model_width))
    route_rows = by_micro(routes[0].reshape(MB, token_rows, 2))
    slot_rows = by_micro(capacity_slots[0].reshape(MB, token_rows, 2))

    norm_columns = jnp.concatenate([ln_gain, ln_bias], axis=1).transpose(0, 2, 1)
    used = 4 * model_width + expert_count + 4
    padding = -used % 128
    packed = jnp.concatenate([w_qkv, w_out, w_router, norm_columns], axis=2)
    packed = jnp.pad(packed, ((0, 0), (0, 0), (0, padding)))
    packed = lax.all_gather(packed, chips, axis=1, tiled=True)
    packed = lax.all_gather(packed, "section", axis=0, tiled=True)
    qkv_all = packed[:, :, : 3 * model_width]
    out_all = packed[:, :, 3 * model_width : 4 * model_width]
    router_all = packed[:, :, 4 * model_width : used - 4]
    norm_all = packed[:, :, used - 4 : used].transpose(0, 2, 1).astype(jnp.float32)
    gain_all = norm_all[:, 0:2]
    shift_all = norm_all[:, 2:4]
    up_all = lax.all_gather(w_up, "section", axis=0, tiled=True)
    down_all = lax.all_gather(w_down, "section", axis=0, tiled=True)

    def tables(expert_ids, slot_ids):
        slot_index = jnp.where(slot_ids < capacity, expert_ids * capacity + slot_ids, -1)
        columns = jnp.arange(expert_count * capacity, dtype=jnp.int32)
        onehot = (slot_index[:, :, None] == columns).astype(half)
        chosen = (expert_ids[:, :, None] == jnp.arange(expert_count, dtype=jnp.int32)).astype(
            jnp.float32
        )
        return (onehot, chosen)

    def to_experts(rows):
        blocks = rows.reshape(expert_count, capacity, model_width)
        arrived = lax.all_to_all(blocks, "expert", split_axis=0, concat_axis=1, tiled=True)
        return lax.all_gather(arrived, "dp", axis=1, tiled=True)

    def from_experts(partial):
        chunks = partial.astype(half).reshape(EXP_DEV, depth, -1, model_width)
        pieces = lax.all_to_all(
            chunks.transpose(1, 0, 2, 3), "dp", split_axis=0, concat_axis=0, tiled=True
        )
        total = jnp.sum(pieces.astype(jnp.float32), axis=0).astype(half)
        blocks = total.reshape(EXP_DEV, groups, capacity, model_width).transpose(1, 0, 2, 3)
        return lax.all_to_all(
            blocks, "expert", split_axis=0, concat_axis=0, tiled=True
        ).reshape(expert_count * capacity, model_width)

    def layer_forward(layer, inputs):
        onehot, chosen = tables(route_rows[layer], slot_rows[layer])
        normed_one, unit_one, inverse_one = norm_forward(
            inputs, gain_all[layer, 0], shift_all[layer, 0]
        )
        norm_one = normed_one.astype(half)
        qkv_rows = jnp.dot(norm_one, qkv_all[layer], preferred_element_type=jnp.float32).astype(half)
        attended, log_totals = attend_forward(qkv_rows, local_images)
        middle = inputs + jnp.dot(attended, out_all[layer], preferred_element_type=jnp.float32)
        normed_two, unit_two, inverse_two = norm_forward(
            middle, gain_all[layer, 1], shift_all[layer, 1]
        )
        norm_two = normed_two.astype(half)
        logits = jnp.dot(norm_two, router_all[layer], preferred_element_type=jnp.float32)
        picked = jnp.sum(logits[:, None, :] * chosen, axis=-1)
        leading = jax.nn.sigmoid(picked[:, 0] - picked[:, 1])
        gate_pair = jnp.stack([leading, 1.0 - leading], axis=-1)
        buffer = jnp.einsum(
            "tjs,td->sd", onehot, norm_two, preferred_element_type=jnp.float32
        ).astype(half)
        all_rows = to_experts(buffer)
        pre_act = jnp.einsum(
            "erd,edf->erf", all_rows, up_all[layer], preferred_element_type=jnp.float32
        )
        hidden = jax.nn.gelu(pre_act, approximate=False).astype(half)
        partial_out = jnp.einsum(
            "erf,efd->erd", hidden, down_all[layer], preferred_element_type=jnp.float32
        )
        back_rows = from_experts(partial_out)
        selected = jnp.einsum(
            "tjs,sd->tjd", onehot, back_rows, preferred_element_type=jnp.float32
        )
        out_rows = middle + jnp.sum(gate_pair[:, :, None] * selected, axis=1)
        saved = (
            inputs, norm_one, qkv_rows, log_totals, attended, middle, norm_two, gate_pair,
            back_rows, all_rows, pre_act, hidden,
        )
        return (out_rows, saved)

    def layer_backward(layer, d_out, saved):
        (
            inputs, norm_one, qkv_rows, log_totals, attended, middle, norm_two, gate_pair,
            back_rows, all_rows, pre_act, hidden,
        ) = saved
        onehot, chosen = tables(route_rows[layer], slot_rows[layer])
        weighted = (gate_pair[:, :, None] * d_out[:, None, :]).astype(half)
        d_buffer = jnp.einsum(
            "tjs,tjd->sd", onehot, weighted, preferred_element_type=jnp.float32
        ).astype(half)
        grads_in = to_experts(d_buffer)
        selected = jnp.einsum("tjs,sd->tjd", onehot, back_rows, preferred_element_type=jnp.float32)
        d_gate = jnp.sum(d_out[:, None, :] * selected, axis=-1)
        d_lead = (d_gate[:, 0] - d_gate[:, 1]) * gate_pair[:, 0] * gate_pair[:, 1]
        d_logits = (d_lead[:, None] * (chosen[:, 0] - chosen[:, 1])).astype(half)
        d_hidden = jnp.einsum(
            "erd,efd->erf", grads_in, down_all[layer], preferred_element_type=jnp.float32
        )
        d_pre = (d_hidden * gelu_slope(pre_act)).astype(half)
        partial_in = jnp.einsum(
            "erf,edf->erd", d_pre, up_all[layer], preferred_element_type=jnp.float32
        )
        d_back = from_experts(partial_in)
        up_grad = jnp.einsum("erd,erf->edf", all_rows, d_pre, preferred_element_type=jnp.float32)
        down_grad = jnp.einsum(
            "erf,erd->efd", hidden, grads_in, preferred_element_type=jnp.float32
        )
        owner_pairs = [(1 - layer, layer)]
        up_sent = lax.ppermute(up_grad.astype(half), "section", owner_pairs)
        down_sent = lax.ppermute(down_grad.astype(half), "section", owner_pairs)
        d_norm_two = jnp.einsum("tjs,sd->td", onehot, d_back, preferred_element_type=jnp.float32)
        d_norm_two = d_norm_two + jnp.einsum(
            "te,de->td", d_logits, router_all[layer], preferred_element_type=jnp.float32
        )
        normed_two, unit_two, inverse_two = norm_forward(
            middle, gain_all[layer, 1], shift_all[layer, 1]
        )
        d_middle_norm, gain_two, shift_two = norm_backward(
            d_norm_two, unit_two, inverse_two, gain_all[layer, 1]
        )
        d_middle = d_out + d_middle_norm
        d_middle_half = d_middle.astype(half)
        d_attended = jnp.einsum(
            "te,de->td", d_middle_half, out_all[layer], preferred_element_type=jnp.float32
        ).astype(half)
        d_qkv = attend_backward(qkv_rows, log_totals, d_attended, local_images)
        d_norm_one = jnp.einsum(
            "te,de->td", d_qkv, qkv_all[layer], preferred_element_type=jnp.float32
        )
        normed_one, unit_one, inverse_one = norm_forward(
            inputs, gain_all[layer, 0], shift_all[layer, 0]
        )
        d_input_norm, gain_one, shift_one = norm_backward(
            d_norm_one, unit_one, inverse_one, gain_all[layer, 0]
        )
        d_input = d_middle + d_input_norm
        operands = [
            lax.ppermute(item, "section", owner_pairs)
            for item in (norm_one, d_qkv, attended, d_middle_half)
        ]
        own = (norm_one, d_qkv, attended, d_middle_half)
        small = jnp.concatenate(
            [
                jnp.einsum("td,te->ed", norm_two, d_logits, preferred_element_type=jnp.float32),
                jnp.stack([gain_one, gain_two, shift_one, shift_two]),
            ]
        )
        small_sent = lax.ppermute(small, "section", owner_pairs)
        small = small + small_sent
        return (d_input, own, operands, small, (up_grad, up_sent), (down_grad, down_sent))

    stream = edge_rows[0]
    saved_list = []
    for layer in range(2):
        if layer > 0:
            stream = stream.astype(half).astype(jnp.float32)
        stream, saved = layer_forward(layer, stream)
        saved_list.append(saved)
    cotangent = edge_rows[1]
    parts = [None, None]
    for layer in (1, 0):
        if layer < 1:
            cotangent = cotangent.astype(half).astype(jnp.float32)
        cotangent, *parts[layer] = layer_backward(layer, cotangent, saved_list[layer])

    def mine(first, second):
        return jnp.where(is_first, first, second)

    own = [mine(a, b) for a, b in zip(parts[0][0], parts[1][0])]
    other = [mine(a, b) for a, b in zip(parts[0][1], parts[1][1])]
    pairs = [jnp.stack([a, b]) for a, b in zip(own, other)]
    qkv_grad = jnp.einsum("ktd,kte->de", pairs[0], pairs[1], preferred_element_type=jnp.float32)
    out_grad = jnp.einsum("ktd,kte->de", pairs[2], pairs[3], preferred_element_type=jnp.float32)
    small_mine = mine(parts[0][2], parts[1][2])

    packed_grad = jnp.concatenate(
        [qkv_grad, out_grad, small_mine.T, jnp.zeros((model_width, padding), jnp.float32)], axis=1
    ).astype(half)
    blocks = packed_grad.reshape(depth, groups, -1, packed_grad.shape[1]).transpose(1, 0, 2, 3)
    blocks = lax.all_to_all(blocks, "expert", split_axis=0, concat_axis=0, tiled=True)
    blocks = jnp.sum(blocks.astype(jnp.float32), axis=0).astype(half)
    blocks = lax.all_to_all(blocks, "dp", split_axis=0, concat_axis=0, tiled=True)
    grad_shard = jnp.sum(blocks.astype(jnp.float32), axis=0)
    norm_shard = grad_shard[:, used - 4 : used].T

    def expert_grad(index):
        first = parts[0][index][0] + parts[0][index][1].astype(jnp.float32)
        second = parts[1][index][0] + parts[1][index][1].astype(jnp.float32)
        return mine(first, second)[None]

    up_shard = expert_grad(3)
    down_shard = expert_grad(4)
    out_sent = lax.ppermute(stream, "section", [(0, 1)])
    grad_sent = lax.ppermute(cotangent, "section", [(1, 0)])
    boundary_rows = mine(jnp.stack([cotangent, grad_sent]), jnp.stack([out_sent, stream]))
    boundary_out = boundary_rows.reshape(1, MB, local_images, boundary_in.shape[3], model_width)
    return (
        boundary_out,
        norm_shard[None, 0:2],
        norm_shard[None, 2:4],
        grad_shard[None, :, : 3 * model_width],
        grad_shard[None, :, 3 * model_width : 4 * model_width],
        grad_shard[None, :, 4 * model_width : used - 4],
        up_shard,
        down_shard,
    )


def solution(mesh):
    in_specs = (
        P("section", None, ("dp", "expert"), None, None),
        P("section", None, ("dp", "expert"), None, None),
        P("section", None, ("dp", "expert"), None, None),
        P("section", None, ("dp", "expert")),
        P("section", None, ("dp", "expert")),
        P("section", ("dp", "expert"), None),
        P("section", ("dp", "expert"), None),
        P("section", ("dp", "expert"), None),
        P("section", "expert", None, "dp"),
        P("section", "expert", "dp", None),
    )
    out_specs = (
        P("section", None, ("dp", "expert"), None, None),
        P("section", None, ("dp", "expert")),
        P("section", None, ("dp", "expert")),
        P("section", ("dp", "expert"), None),
        P("section", ("dp", "expert"), None),
        P("section", ("dp", "expert"), None),
        P("section", "expert", None, "dp"),
        P("section", "expert", "dp", None),
    )
    return jax.shard_map(
        on_device, mesh=mesh, in_specs=in_specs, out_specs=out_specs, check_vma=False
    )
```

```python
import math

import jax
import jax.numpy as jnp
from jax import lax
from jax.sharding import PartitionSpec as P

HEADS = 12
HEAD_DIM = 64
EXP_DEV = 2
MB = 2


EPS = 1e-06
SQRT_HALF = 0.7071067811865476
INV_ROOT_TAU = 0.3989422804014327


def norm_forward(values, gain_row, shift_row):
    centred = values - jnp.mean(values, axis=-1, keepdims=True)
    variance = jnp.mean(centred * centred, axis=-1, keepdims=True)
    inverse = lax.rsqrt(variance + EPS)
    unit_rows = centred * inverse
    return (unit_rows * gain_row + shift_row, unit_rows, inverse)


def norm_backward(d_normed, unit_rows, inverse, gain_row):
    d_gain = jnp.sum(d_normed * unit_rows, axis=0)
    d_shift = jnp.sum(d_normed, axis=0)
    scaled = d_normed * gain_row
    d_values = inverse * (
        scaled
        - jnp.mean(scaled, axis=-1, keepdims=True)
        - unit_rows * jnp.mean(scaled * unit_rows, axis=-1, keepdims=True)
    )
    return (d_values, d_gain, d_shift)


def gelu_slope(pre_act):
    return (
        0.5 * (1.0 + lax.erf(pre_act * SQRT_HALF))
        + pre_act * jnp.exp(-0.5 * pre_act * pre_act) * INV_ROOT_TAU
    )


def split_heads(qkv_rows, image_count):
    feature_count = qkv_rows.shape[1] // 3
    return [
        qkv_rows[:, part_index * feature_count : (part_index + 1) * feature_count].reshape(
            image_count, -1, HEADS, HEAD_DIM
        )
        for part_index in range(3)
    ]


def attend_forward(qkv_rows, image_count):
    queries, key_rows, value_rows = split_heads(qkv_rows, image_count)
    scale_factor = 1.0 / math.sqrt(HEAD_DIM)
    scores = (
        jnp.einsum("bqhd,bkhd->bhqk", queries, key_rows, preferred_element_type=jnp.float32)
        * scale_factor
    )
    log_totals = jnp.log(jnp.sum(jnp.exp(scores), axis=-1))
    probs_half = jnp.exp(scores - log_totals[..., None]).astype(jnp.bfloat16)
    attended = jnp.einsum(
        "bhqk,bkhd->bqhd", probs_half, value_rows, preferred_element_type=jnp.float32
    )
    return (attended.astype(jnp.bfloat16).reshape(-1, HEADS * HEAD_DIM), log_totals)


def attend_backward(qkv_rows, log_totals, d_attended, image_count):
    queries, key_rows, value_rows = split_heads(qkv_rows, image_count)
    scale_factor = 1.0 / math.sqrt(HEAD_DIM)
    scores = (
        jnp.einsum("bqhd,bkhd->bhqk", queries, key_rows, preferred_element_type=jnp.float32)
        * scale_factor
    )
    probs = jnp.exp(scores - log_totals[..., None])
    probs_half = probs.astype(jnp.bfloat16)
    d_heads = d_attended.reshape(image_count, -1, HEADS, HEAD_DIM)
    d_values = jnp.einsum(
        "bhqk,bqhd->bkhd", probs_half, d_heads, preferred_element_type=jnp.float32
    )
    d_probs = jnp.einsum("bqhd,bkhd->bhqk", d_heads, value_rows, preferred_element_type=jnp.float32)
    row_dot = jnp.sum(probs * d_probs, axis=-1, keepdims=True)
    d_scores = (probs * (d_probs - row_dot) * scale_factor).astype(jnp.bfloat16)
    d_queries = jnp.einsum(
        "bhqk,bkhd->bqhd", d_scores, key_rows, preferred_element_type=jnp.float32
    )
    d_keys = jnp.einsum("bhqk,bqhd->bkhd", d_scores, queries, preferred_element_type=jnp.float32)
    feature_count = HEADS * HEAD_DIM
    joined = jnp.concatenate(
        [
            d_queries.reshape(-1, feature_count),
            d_keys.reshape(-1, feature_count),
            d_values.reshape(-1, feature_count),
        ],
        axis=1,
    )
    return joined.astype(jnp.bfloat16)


def on_device(
    boundary_in, routes, capacity_slots, ln_gain, ln_bias, w_qkv, w_out, w_router, w_up, w_down
):
    section_index = lax.axis_index("section")
    is_first = section_index == 0
    depth = lax.axis_size("dp")
    groups = lax.axis_size("expert")
    expert_count = EXP_DEV * groups
    local_images = boundary_in.shape[2]
    token_rows = local_images * boundary_in.shape[3]
    model_width = boundary_in.shape[4]
    capacity = 26 * token_rows // (16 * expert_count)
    chips = ("dp", "expert")
    half = jnp.bfloat16

    def by_micro(values):
        return lax.all_to_all(values, "section", split_axis=0, concat_axis=0, tiled=True)

    edge_rows = by_micro(boundary_in[0].reshape(MB, token_rows, model_width))
    route_rows = by_micro(routes[0].reshape(MB, token_rows, 2))
    slot_rows = by_micro(capacity_slots[0].reshape(MB, token_rows, 2))

    norm_columns = jnp.concatenate([ln_gain, ln_bias], axis=1).transpose(0, 2, 1)
    used = 4 * model_width + expert_count + 4
    padding = -used % 128
    packed = jnp.concatenate([w_qkv, w_out, w_router, norm_columns], axis=2)
    packed = jnp.pad(packed, ((0, 0), (0, 0), (0, padding)))
    halves = by_micro(packed[0].reshape(2, -1, packed.shape[2]))
    qkv_all, out_all, router_all, gain_all, shift_all = [], [], [], [], []

    def gather_layer(shard):
        part = lax.all_gather(shard[None], chips, axis=0, tiled=True)
        whole = lax.all_gather(part, "section", axis=1).reshape(model_width, -1)
        norm_rows = whole[:, used - 4 : used].T.astype(jnp.float32)
        qkv_all.append(whole[:, : 3 * model_width])
        out_all.append(whole[:, 3 * model_width : 4 * model_width])
        router_all.append(whole[:, 4 * model_width : used - 4])
        gain_all.append(norm_rows[0:2])
        shift_all.append(norm_rows[2:4])

    gather_layer(halves[0])
    up_all = lax.all_gather(w_up, "section", axis=0, tiled=True)
    down_all = lax.all_gather(w_down, "section", axis=0, tiled=True)

    def tables(expert_ids, slot_ids):
        slot_index = jnp.where(slot_ids < capacity, expert_ids * capacity + slot_ids, -1)
        columns = jnp.arange(expert_count * capacity, dtype=jnp.int32)
        onehot = (slot_index[:, :, None] == columns).astype(half)
        chosen = (expert_ids[:, :, None] == jnp.arange(expert_count, dtype=jnp.int32)).astype(
            jnp.float32
        )
        return (onehot, chosen)

    def to_experts(rows):
        blocks = rows.reshape(expert_count, capacity, model_width)
        arrived = lax.all_to_all(blocks, "expert", split_axis=0, concat_axis=1, tiled=True)
        return lax.all_gather(arrived, "dp", axis=1, tiled=True)

    def from_experts(partial):
        chunks = partial.astype(half).reshape(EXP_DEV, depth, -1, model_width)
        pieces = lax.all_to_all(
            chunks.transpose(1, 0, 2, 3), "dp", split_axis=0, concat_axis=0, tiled=True
        )
        total = jnp.sum(pieces.astype(jnp.float32), axis=0).astype(half)
        blocks = total.reshape(EXP_DEV, groups, capacity, model_width).transpose(1, 0, 2, 3)
        return lax.all_to_all(
            blocks, "expert", split_axis=0, concat_axis=0, tiled=True
        ).reshape(expert_count * capacity, model_width)

    def layer_forward(layer, inputs):
        onehot, chosen = tables(route_rows[layer], slot_rows[layer])
        normed_one, unit_one, inverse_one = norm_forward(
            inputs, gain_all[layer][0], shift_all[layer][0]
        )
        norm_one = normed_one.astype(half)
        qkv_rows = jnp.dot(norm_one, qkv_all[layer], preferred_element_type=jnp.float32).astype(half)
        attended, log_totals = attend_forward(qkv_rows, local_images)
        middle = inputs + jnp.dot(attended, out_all[layer], preferred_element_type=jnp.float32)
        normed_two, unit_two, inverse_two = norm_forward(
            middle, gain_all[layer][1], shift_all[layer][1]
        )
        norm_two = normed_two.astype(half)
        logits = jnp.dot(norm_two, router_all[layer], preferred_element_type=jnp.float32)
        picked = jnp.sum(logits[:, None, :] * chosen, axis=-1)
        leading = jax.nn.sigmoid(picked[:, 0] - picked[:, 1])
        gate_pair = jnp.stack([leading, 1.0 - leading], axis=-1)
        buffer = jnp.einsum(
            "tjs,td->sd", onehot, norm_two, preferred_element_type=jnp.float32
        ).astype(half)
        all_rows = to_experts(buffer)
        pre_act = jnp.einsum(
            "erd,edf->erf", all_rows, up_all[layer], preferred_element_type=jnp.float32
        )
        hidden = jax.nn.gelu(pre_act, approximate=False).astype(half)
        partial_out = jnp.einsum(
            "erf,efd->erd", hidden, down_all[layer], preferred_element_type=jnp.float32
        )
        back_rows = from_experts(partial_out)
        selected = jnp.einsum(
            "tjs,sd->tjd", onehot, back_rows, preferred_element_type=jnp.float32
        )
        out_rows = middle + jnp.sum(gate_pair[:, :, None] * selected, axis=1)
        saved = (
            inputs, norm_one, qkv_rows, log_totals, attended, middle, norm_two, gate_pair,
            back_rows, all_rows, pre_act, hidden,
        )
        return (out_rows, saved)

    def layer_backward(layer, d_out, saved):
        (
            inputs, norm_one, qkv_rows, log_totals, attended, middle, norm_two, gate_pair,
            back_rows, all_rows, pre_act, hidden,
        ) = saved
        onehot, chosen = tables(route_rows[layer], slot_rows[layer])
        weighted = (gate_pair[:, :, None] * d_out[:, None, :]).astype(half)
        d_buffer = jnp.einsum(
            "tjs,tjd->sd", onehot, weighted, preferred_element_type=jnp.float32
        ).astype(half)
        grads_in = to_experts(d_buffer)
        selected = jnp.einsum("tjs,sd->tjd", onehot, back_rows, preferred_element_type=jnp.float32)
        d_gate = jnp.sum(d_out[:, None, :] * selected, axis=-1)
        d_lead = (d_gate[:, 0] - d_gate[:, 1]) * gate_pair[:, 0] * gate_pair[:, 1]
        d_logits = (d_lead[:, None] * (chosen[:, 0] - chosen[:, 1])).astype(half)
        d_hidden = jnp.einsum(
            "erd,efd->erf", grads_in, down_all[layer], preferred_element_type=jnp.float32
        )
        d_pre = (d_hidden * gelu_slope(pre_act)).astype(half)
        partial_in = jnp.einsum(
            "erf,edf->erd", d_pre, up_all[layer], preferred_element_type=jnp.float32
        )
        d_back = from_experts(partial_in)
        up_grad = jnp.einsum("erd,erf->edf", all_rows, d_pre, preferred_element_type=jnp.float32)
        down_grad = jnp.einsum(
            "erf,erd->efd", hidden, grads_in, preferred_element_type=jnp.float32
        )
        owner_pairs = [(1 - layer, layer)]
        up_sent = lax.ppermute(up_grad.astype(half), "section", owner_pairs)
        down_sent = lax.ppermute(down_grad.astype(half), "section", owner_pairs)
        d_norm_two = jnp.einsum("tjs,sd->td", onehot, d_back, preferred_element_type=jnp.float32)
        d_norm_two = d_norm_two + jnp.einsum(
            "te,de->td", d_logits, router_all[layer], preferred_element_type=jnp.float32
        )
        normed_two, unit_two, inverse_two = norm_forward(
            middle, gain_all[layer][1], shift_all[layer][1]
        )
        d_middle_norm, gain_two, shift_two = norm_backward(
            d_norm_two, unit_two, inverse_two, gain_all[layer][1]
        )
        d_middle = d_out + d_middle_norm
        d_middle_half = d_middle.astype(half)
        d_attended = jnp.einsum(
            "te,de->td", d_middle_half, out_all[layer], preferred_element_type=jnp.float32
        ).astype(half)
        d_qkv = attend_backward(qkv_rows, log_totals, d_attended, local_images)
        d_norm_one = jnp.einsum(
            "te,de->td", d_qkv, qkv_all[layer], preferred_element_type=jnp.float32
        )
        normed_one, unit_one, inverse_one = norm_forward(
            inputs, gain_all[layer][0], shift_all[layer][0]
        )
        d_input_norm, gain_one, shift_one = norm_backward(
            d_norm_one, unit_one, inverse_one, gain_all[layer][0]
        )
        d_input = d_middle + d_input_norm
        operands = [
            lax.ppermute(item, "section", owner_pairs)
            for item in (norm_one, d_qkv, attended, d_middle_half)
        ]
        own = (norm_one, d_qkv, attended, d_middle_half)
        small = jnp.concatenate(
            [
                jnp.einsum("td,te->ed", norm_two, d_logits, preferred_element_type=jnp.float32),
                jnp.stack([gain_one, gain_two, shift_one, shift_two]),
            ]
        )
        small_sent = lax.ppermute(small, "section", owner_pairs)
        small = small + small_sent
        return (d_input, own, operands, small, (up_grad, up_sent), (down_grad, down_sent))

    stream = edge_rows[0]
    saved_list = []
    for layer in range(2):
        if layer > 0:
            stream = stream.astype(half).astype(jnp.float32)
            gather_layer(lax.optimization_barrier((halves[1], saved_list[0][9]))[0])
        stream, saved = layer_forward(layer, stream)
        saved_list.append(saved)
    cotangent = edge_rows[1]
    parts = [None, None]
    for layer in (1, 0):
        if layer < 1:
            cotangent = cotangent.astype(half).astype(jnp.float32)
        cotangent, *parts[layer] = layer_backward(layer, cotangent, saved_list[layer])

    def mine(first, second):
        return jnp.where(is_first, first, second)

    own = [mine(a, b) for a, b in zip(parts[0][0], parts[1][0])]
    other = [mine(a, b) for a, b in zip(parts[0][1], parts[1][1])]
    pairs = [jnp.stack([a, b]) for a, b in zip(own, other)]
    qkv_grad = jnp.einsum("ktd,kte->de", pairs[0], pairs[1], preferred_element_type=jnp.float32)
    out_grad = jnp.einsum("ktd,kte->de", pairs[2], pairs[3], preferred_element_type=jnp.float32)
    small_mine = mine(parts[0][2], parts[1][2])

    packed_grad = jnp.concatenate(
        [qkv_grad, out_grad, small_mine.T, jnp.zeros((model_width, padding), jnp.float32)], axis=1
    ).astype(half)
    blocks = packed_grad.reshape(depth, groups, -1, packed_grad.shape[1]).transpose(1, 0, 2, 3)
    blocks = lax.all_to_all(blocks, "expert", split_axis=0, concat_axis=0, tiled=True)
    blocks = jnp.sum(blocks.astype(jnp.float32), axis=0).astype(half)
    blocks = lax.all_to_all(blocks, "dp", split_axis=0, concat_axis=0, tiled=True)
    grad_shard = jnp.sum(blocks.astype(jnp.float32), axis=0)
    norm_shard = grad_shard[:, used - 4 : used].T

    def expert_grad(index):
        first = parts[0][index][0] + parts[0][index][1].astype(jnp.float32)
        second = parts[1][index][0] + parts[1][index][1].astype(jnp.float32)
        return mine(first, second)[None]

    up_shard = expert_grad(3)
    down_shard = expert_grad(4)
    out_sent = lax.ppermute(stream, "section", [(0, 1)])
    grad_sent = lax.ppermute(cotangent, "section", [(1, 0)])
    boundary_rows = mine(jnp.stack([cotangent, grad_sent]), jnp.stack([out_sent, stream]))
    boundary_out = boundary_rows.reshape(1, MB, local_images, boundary_in.shape[3], model_width)
    return (
        boundary_out,
        norm_shard[None, 0:2],
        norm_shard[None, 2:4],
        grad_shard[None, :, : 3 * model_width],
        grad_shard[None, :, 3 * model_width : 4 * model_width],
        grad_shard[None, :, 4 * model_width : used - 4],
        up_shard,
        down_shard,
    )


def solution(mesh):
    in_specs = (
        P("section", None, ("dp", "expert"), None, None),
        P("section", None, ("dp", "expert"), None, None),
        P("section", None, ("dp", "expert"), None, None),
        P("section", None, ("dp", "expert")),
        P("section", None, ("dp", "expert")),
        P("section", ("dp", "expert"), None),
        P("section", ("dp", "expert"), None),
        P("section", ("dp", "expert"), None),
        P("section", "expert", None, "dp"),
        P("section", "expert", "dp", None),
    )
    out_specs = (
        P("section", None, ("dp", "expert"), None, None),
        P("section", None, ("dp", "expert")),
        P("section", None, ("dp", "expert")),
        P("section", ("dp", "expert"), None),
        P("section", ("dp", "expert"), None),
        P("section", ("dp", "expert"), None),
        P("section", "expert", None, "dp"),
        P("section", "expert", "dp", None),
    )
    return jax.shard_map(
        on_device, mesh=mesh, in_specs=in_specs, out_specs=out_specs, check_vma=False
    )
```
